256 devices in a mesh: seq: 64 (over z, y, core), head: 4 (over x).
Axes of the slice: x: 4, y: 4, z: 8, core: 2. Of those that a mesh axis runs over, the one named last changes fastest.
Arguments:
- rotated_query_rows: bfloat16 [32768, 4096], P(('seq', 'head')), may hold values from -8 to 8
- rotated_key_rows: bfloat16 [32768, 2048], P(('seq', 'head')), may hold values from -8 to 8
- value_matrix: bfloat16 [32768, 2048], P(('seq', 'head')), may hold values from -6 to 6
- output_gradient: bfloat16 [32768, 4096], P(('seq', 'head')), may hold values from -6 to 6
- doc_lengths: int32 [64], replicated, may hold values from 1 to 2048, 32768 in all
Outputs:
- attended: bfloat16 [32768, 4096], P(('seq', 'head'))
- query_grad: bfloat16 [32768, 4096], P(('seq', 'head'))
- key_gradient: bfloat16 [32768, 2048], P(('seq', 'head'))
- value_gradient: bfloat16 [32768, 2048], P(('seq', 'head'))
The draws below stay inside these ranges and needn't reach their ends.
Inputs may be any that keep to these rules, and one draw needn't show every extreme that they name: `doc_lengths`: the lengths of the 64 documents packed in order; they sum to 32768 and the longest has 2048 tokens.
All inputs are finite; a program needn't handle non-finite values.
Results may differ from the reference program's by a relative error of at most 0.02.
Values may be sent and summed in bfloat16 or wider, within the bound.
A program may use at most 128 MiB of HBM per device.

```python
import math
import jax
import jax.numpy as jnp
import numpy as np
from jax import lax

QUERY_HEADS = 16
KEY_VALUE_HEADS = 8
HEAD_WIDTH = 256
WINDOW_LENGTH = 1024
MOST_DOC = 2048
STREAM_TOKENS = 32768
DOCS = 64


def draw_rotated_query_rows(key, part):
    own_key = jax.random.fold_in(key, 1)
    column_positions = QUERY_HEADS * HEAD_WIDTH
    drawn = jnp.clip(jax.random.normal(own_key, (STREAM_TOKENS, column_positions)), -6.0, 6.0)
    return drawn.astype(jnp.bfloat16)


def draw_rotated_key_rows(key, part):
    own_key = jax.random.fold_in(key, 2)
    column_positions = KEY_VALUE_HEADS * HEAD_WIDTH
    drawn = jnp.clip(jax.random.normal(own_key, (STREAM_TOKENS, column_positions)), -6.0, 6.0)
    return drawn.astype(jnp.bfloat16)


def levels(key, dims, shards, low, high):
    gain, own = 1.0, jax.random.fold_in(key, 6)
    for position, blocks in shards:
        heights = jnp.exp(jax.random.uniform(jax.random.fold_in(own, position), (blocks,), jnp.float32, low / len(shards), high / len(shards)))
        gain = gain * jnp.repeat(heights, dims[position] // blocks).reshape([-1 if axis == position else 1 for axis in range(len(dims))])
    return gain


def split_up(amount, total, reach, lean):
    portions = [(1 << 20) // math.isqrt(rank ** lean) + 1 for rank in range(2, amount + 1)]
    rest, holding = total - reach - (amount - 1), [1] * (amount - 1)
    while rest > 0:
        candidates = [i for i in range(amount - 1) if holding[i] < reach]
        pool, remaining = sum([portions[i] for i in candidates]), rest
        for i in candidates:
            extra = min(reach - holding[i], max(1, remaining * portions[i] // pool), rest)
            holding[i] = holding[i] + extra
            rest = rest - extra
    return np.array([reach] + holding)


def uneven_parts(rng, amount, total, limit, slope):
    if amount == 2:
        one = jax.random.randint(rng, (), max(1, total - limit), min(limit, total - 1) + 1)
        return jnp.stack([one, total - one])
    tallies = jnp.asarray(split_up(amount, total, limit, slope), jnp.int32)
    couples = (amount - 1) // 2
    donor, receiver = tallies[1:1 + 2 * couples:2], tallies[2:2 + 2 * couples:2]
    slack = jnp.minimum(donor - 1, limit - receiver)
    moved = jax.random.randint(jax.random.fold_in(rng, 1), (couples,), 0, 1 << 20) % (slack + 1)
    tallies = tallies.at[1:1 + 2 * couples:2].set(donor - moved).at[2:2 + 2 * couples:2].set(receiver + moved)
    return tallies[jax.random.permutation(jax.random.fold_in(rng, 2), amount)]


def bell_draw(key, shape, spread, bound, shards=(), held_as=jnp.bfloat16):
    loudness = levels(key, shape, shards, -0.22, 0.18) if shards else 1.0
    result = jax.random.normal(key, shape, jnp.float32) * spread * loudness
    return jnp.minimum(jnp.maximum(result, -bound), bound).astype(held_as)


def setup_inputs(seed: int = 0) -> dict:
    seeds = jax.random.split(jax.random.key(seed), 6)
    rotated_query_rows = draw_rotated_query_rows(jax.random.fold_in(seeds[5], 71), 0)
    rotated_key_rows = draw_rotated_key_rows(jax.random.fold_in(seeds[5], 71), 0)
    value_matrix = bell_draw(seeds[2], (STREAM_TOKENS, KEY_VALUE_HEADS * HEAD_WIDTH), 1.0, 6.0, ((0, 256),))
    output_gradient = bell_draw(seeds[3], (STREAM_TOKENS, QUERY_HEADS * HEAD_WIDTH), 1.0, 6.0, ((0, 256),))
    doc_lengths = uneven_parts(seeds[4], DOCS, STREAM_TOKENS, MOST_DOC, 2).astype(jnp.int32)
    return dict(rotated_query_rows=rotated_query_rows, rotated_key_rows=rotated_key_rows, value_matrix=value_matrix, output_gradient=output_gradient, doc_lengths=doc_lengths)


def doc_index(positions, doc_lengths):
    starts = jnp.cumsum(doc_lengths) - doc_lengths
    counted = jnp.sum((starts[None, :] <= positions[:, None]).astype(jnp.int32), axis=1)
    return (counted - 1).astype(jnp.int32)


def reference(rotated_query_rows, rotated_key_rows, value_matrix, output_gradient, doc_lengths):
    token_total = rotated_query_rows.shape[0]
    group_width = QUERY_HEADS // KEY_VALUE_HEADS
    score_scale = HEAD_WIDTH ** -0.5
    key_span = 2 * WINDOW_LENGTH
    query_head_count = rotated_query_rows.reshape(token_total, KEY_VALUE_HEADS, group_width, HEAD_WIDTH)
    gradient_heads = output_gradient.reshape(token_total, KEY_VALUE_HEADS, group_width, HEAD_WIDTH)
    leading_padding = jnp.zeros((WINDOW_LENGTH, KEY_VALUE_HEADS, HEAD_WIDTH), jnp.bfloat16)
    key_head_count = jnp.concatenate([leading_padding, rotated_key_rows.reshape(token_total, KEY_VALUE_HEADS, HEAD_WIDTH)], axis=0)
    value_head_count = jnp.concatenate([leading_padding, value_matrix.reshape(token_total, KEY_VALUE_HEADS, HEAD_WIDTH)], axis=0)
    documents = doc_index(jnp.arange(-WINDOW_LENGTH, token_total, dtype=jnp.int32), doc_lengths)
    offsets = (jnp.arange(WINDOW_LENGTH, dtype=jnp.int32) + WINDOW_LENGTH)[:, None] - jnp.arange(key_span, dtype=jnp.int32)[None, :]

    def tile_step(carried, tile_index):
        key_gradient_sums, value_gradient_sums = carried
        first_row = (tile_index * WINDOW_LENGTH).astype(jnp.int32)
        query_tile = lax.dynamic_slice_in_dim(query_head_count, first_row, WINDOW_LENGTH, 0).astype(jnp.float32)
        grad_tile = lax.dynamic_slice_in_dim(gradient_heads, first_row, WINDOW_LENGTH, 0).astype(jnp.float32)
        key_tile = lax.dynamic_slice_in_dim(key_head_count, first_row, key_span, 0).astype(jnp.float32)
        value_tile = lax.dynamic_slice_in_dim(value_head_count, first_row, key_span, 0).astype(jnp.float32)
        query_docs = lax.dynamic_slice_in_dim(documents, first_row + WINDOW_LENGTH, WINDOW_LENGTH, 0)
        key_docs = lax.dynamic_slice_in_dim(documents, first_row, key_span, 0)
        visible = (query_docs[:, None] == key_docs[None, :]) & (offsets >= 0) & (offsets < WINDOW_LENGTH)
        scores = jnp.einsum("qhgd,khd->hgqk", query_tile, key_tile) * score_scale
        scores = jnp.where(visible[None, None], scores, -jnp.inf)
        row_max = jnp.max(scores, axis=3, keepdims=True)
        weights = jnp.exp(scores - row_max)
        probs_full = weights / jnp.sum(weights, axis=3, keepdims=True)
        probs_low = lax.optimization_barrier(probs_full.astype(jnp.bfloat16)).astype(jnp.float32)
        attended = jnp.einsum("hgqk,khd->qhgd", probs_low, value_tile).astype(jnp.bfloat16)
        row_delta = jnp.sum(grad_tile * attended.astype(jnp.float32), axis=3)
        value_part = jnp.einsum("hgqk,qhgd->khd", probs_low, grad_tile)
        grad_probs = jnp.einsum("qhgd,khd->hgqk", grad_tile, value_tile)
        grad_scores = probs_full * (grad_probs - jnp.transpose(row_delta, (1, 2, 0))[..., None])
        grad_low = lax.optimization_barrier(grad_scores.astype(jnp.bfloat16)).astype(jnp.float32)
        query_grad = (jnp.einsum("hgqk,khd->qhgd", grad_low, key_tile) * score_scale).astype(jnp.bfloat16)
        key_part = jnp.einsum("hgqk,qhgd->khd", grad_low, query_tile) * score_scale
        key_gradient_sums = lax.dynamic_update_slice_in_dim(
            key_gradient_sums, lax.dynamic_slice_in_dim(key_gradient_sums, first_row, key_span, 0) + key_part, first_row, 0)
        value_gradient_sums = lax.dynamic_update_slice_in_dim(
            value_gradient_sums, lax.dynamic_slice_in_dim(value_gradient_sums, first_row, key_span, 0) + value_part, first_row, 0)
        return (key_gradient_sums, value_gradient_sums), (attended, query_grad)

    vacant_sums = jnp.zeros((token_total + WINDOW_LENGTH, KEY_VALUE_HEADS, HEAD_WIDTH), jnp.float32)
    (key_gradient_sums, value_gradient_sums), (attended, query_grad) = lax.scan(
        tile_step, (vacant_sums, vacant_sums), jnp.arange(token_total // WINDOW_LENGTH, dtype=jnp.int32))
    attended = attended.reshape(token_total, QUERY_HEADS * HEAD_WIDTH)
    query_grad = query_grad.reshape(token_total, QUERY_HEADS * HEAD_WIDTH)
    key_gradient = key_gradient_sums[WINDOW_LENGTH:].astype(jnp.bfloat16).reshape(token_total, KEY_VALUE_HEADS * HEAD_WIDTH)
    value_gradient = value_gradient_sums[WINDOW_LENGTH:].astype(jnp.bfloat16).reshape(token_total, KEY_VALUE_HEADS * HEAD_WIDTH)
    return (attended, query_grad, key_gradient, value_gradient)
```

```python
import functools
import math

import jax
import jax.numpy as jnp
from jax import lax
from jax.experimental import pallas as pl
from jax.experimental.pallas import tpu as pltpu
from jax.sharding import PartitionSpec as P

MESH = pl.DeviceIdType.MESH
HEAD_WIDTH = 256
WINDOW = 1024
TILE = 256
SPAN = WINDOW + TILE
SCALE = HEAD_WIDTH ** -0.5
LOG2E = math.log2(math.e)
HIDDEN = -1e30
NT = (((1,), (1,)), ((), ()))
NN = (((1,), (0,)), ((), ()))
TN = (((0,), (0,)), ((), ()))


def dot(left, right, dims):
    return lax.dot_general(left, right, dims, preferred_element_type=jnp.float32)


def kernel(
    chips,
    block,
    group,
    q_hbm,
    k_hbm,
    v_hbm,
    g_hbm,
    lens,
    o_hbm,
    dq_hbm,
    dk_hbm,
    dv_hbm,
    q_own,
    g_own,
    k_win,
    v_win,
    o_own,
    dq_own,
    probs,
    first_key,
    dk_sum,
    dv_sum,
    rim_dk,
    rim_dv,
    back_dk,
    back_dv,
    dk_own,
    dv_own,
    in_send,
    in_recv,
    rim_send,
    rim_recv,
    back_send,
    back_recv,
    out_send,
    out_recv,
):
    blocks = 2 * chips
    rows = blocks * block
    tiles = rows // TILE
    per_tile = TILE // block
    wide = group * HEAD_WIDTH
    seq = lax.axis_index("seq")
    x = lax.axis_index("head")
    seqs = lax.axis_size("seq")
    core = lax.rem(seq, 2)
    row_base = seq - core
    mine = core * chips + x
    head = 2 * x + core
    after = (lax.rem(seq + 2, seqs), x)
    before = (lax.rem(seq + seqs - 2, seqs), x)

    peers = []
    for dx, dc in ((0, 1), (1, 0), (chips - 1, 0), (1, 1), (chips - 1, 1), (2, 0), (2, 1)):
        peer_core = lax.rem(core + dc, 2)
        peer_x = lax.rem(x + dx, chips)
        peers.append((row_base + peer_core, peer_x, peer_core * chips + peer_x, 2 * peer_x + peer_core))

    barrier = pltpu.get_barrier_semaphore()
    for peer in peers:
        pl.semaphore_signal(barrier, inc=1, device_id=(peer[0], peer[1]), device_id_type=MESH)
    pl.semaphore_signal(barrier, inc=1, device_id=after, device_id_type=MESH)
    pl.semaphore_signal(barrier, inc=1, device_id=before, device_id_type=MESH)

    def block_rows(index, offset=0):
        return pl.ds(pl.multiple_of(offset + index * block, block), block)

    def head_columns(index, width):
        return pl.ds(pl.multiple_of(index * width, width), width)

    moves = (
        (k_hbm, k_win, HEAD_WIDTH, WINDOW),
        (v_hbm, v_win, HEAD_WIDTH, WINDOW),
        (q_hbm, q_own, wide, 0),
        (g_hbm, g_own, wide, 0),
    )
    for a, (source, target, width, offset) in enumerate(moves):
        pltpu.make_async_copy(
            source.at[:, head_columns(head, width)],
            target.at[block_rows(mine, offset), :],
            in_recv.at[a, mine],
        ).start()

    place = (seq // 2) * rows + lax.broadcasted_iota(jnp.int32, (8, rows), 1)

    def next_doc(d, carry):
        start, first = carry
        return start + lens[d], jnp.where(place >= start, start, first)

    _, first = lax.fori_loop(
        0, lens.shape[0], next_doc, (jnp.int32(0), jnp.zeros((8, rows), jnp.int32))
    )
    in_row = lax.broadcasted_iota(jnp.int32, (8, rows), 1)
    tile_start = in_row // TILE * TILE
    first = jnp.maximum(first, place - (WINDOW - 1)) - (place - in_row - WINDOW) - tile_start
    first_key[...] = jnp.transpose(jnp.concatenate([first] * 16, axis=0))
    dk_sum[...] = jnp.zeros_like(dk_sum)
    dv_sum[...] = jnp.zeros_like(dv_sum)

    pl.semaphore_wait(barrier, len(peers) + 2)

    sends = []
    for a, (source, target, width, offset) in enumerate(moves):
        for n, peer in enumerate(peers):
            copy = pltpu.make_async_remote_copy(
                src_ref=source.at[:, head_columns(peer[3], width)],
                dst_ref=target.at[block_rows(mine, offset), :],
                send_sem=in_send.at[a, n],
                recv_sem=in_recv.at[a, mine],
                device_id=(peer[0], peer[1]),
                device_id_type=MESH,
            )
            copy.start()
            sends.append(copy)

    def arrived(a, index):
        source, target, width, offset = moves[a]
        landed = target.at[block_rows(index, offset), :]
        pltpu.make_async_copy(landed, landed, in_recv.at[a, index]).wait()

    for index in [mine] + [peer[2] for peer in peers]:
        for a, window in ((0, k_win), (1, v_win)):
            arrived(a, index)
            copy = pltpu.make_async_remote_copy(
                src_ref=window.at[block_rows(index, WINDOW), :],
                dst_ref=window.at[block_rows(index), :],
                send_sem=rim_send.at[a, index],
                recv_sem=rim_recv.at[a, index],
                device_id=after,
                device_id_type=MESH,
            )
            copy.start()
            sends.append(copy)

    for index in range(blocks):
        arrived(2, index)
    for index in range(blocks):
        for a, window in ((0, k_win), (1, v_win)):
            landed = window.at[block_rows(index), :]
            pltpu.make_async_copy(landed, landed, rim_recv.at[a, index]).wait()

    def send_home(a, source, target, width, index):
        owner = (row_base + index // chips, lax.rem(index, chips))

        @pl.when(index == mine)
        def _():
            pltpu.make_async_copy(
                source.at[block_rows(index), :],
                target.at[:, head_columns(head, width)],
                out_recv.at[a, head],
            ).start()

        @pl.when(index != mine)
        def _():
            pltpu.make_async_remote_copy(
                src_ref=source.at[block_rows(index), :],
                dst_ref=target.at[:, head_columns(head, width)],
                send_sem=out_send.at[a, index],
                recv_sem=out_recv.at[a, head],
                device_id=owner,
                device_id_type=MESH,
            ).start()

    column = lax.broadcasted_iota(jnp.int32, (TILE, SPAN), 1)
    last_key = lax.broadcasted_iota(jnp.int32, (TILE, SPAN), 0) + WINDOW

    @pl.loop(0, tiles)
    def _(t):
        at = pl.multiple_of(t * TILE, TILE)
        keys = pl.ds(at, SPAN)
        for g in range(group):
            columns = slice(g * HEAD_WIDTH, (g + 1) * HEAD_WIDTH)
            scores = dot(q_own[pl.ds(at, TILE), columns], k_win[keys, :], NT)
            visible = (column >= first_key[pl.ds(at, TILE), 0:1]) & (column <= last_key)
            scores = jnp.where(visible, scores, HIDDEN)
            top = jnp.max(scores, axis=1, keepdims=True)
            weights = jnp.exp2((scores - top) * (SCALE * LOG2E))
            total = jnp.sum(weights, axis=1, keepdims=True)
            probs_low = (weights * (1.0 / total)).astype(jnp.bfloat16)
            probs[t, g * TILE : (g + 1) * TILE, :] = probs_low
            o_own[pl.ds(at, TILE), columns] = dot(probs_low, v_win[keys, :], NN).astype(jnp.bfloat16)
        for n in range(per_tile):
            send_home(0, o_own, o_hbm, wide, t * per_tile + n)

    for index in range(blocks):
        arrived(3, index)

    def summed(sums, chunk_start, scale):
        chunk = jnp.transpose(sums[:, pl.ds(chunk_start, TILE)])
        return chunk * scale if scale is not None else chunk

    @pl.loop(0, tiles)
    def _(t):
        at = pl.multiple_of(t * TILE, TILE)
        keys = pl.ds(at, SPAN)
        for g in range(group):
            columns = slice(g * HEAD_WIDTH, (g + 1) * HEAD_WIDTH)
            query = q_own[pl.ds(at, TILE), columns]
            grad = g_own[pl.ds(at, TILE), columns]
            low = o_own[pl.ds(at, TILE), columns]
            delta = jnp.sum(grad.astype(jnp.float32) * low.astype(jnp.float32), axis=1, keepdims=True)
            probs_low = probs[t, g * TILE : (g + 1) * TILE, :]
            dv_sum[:, keys] += dot(grad, probs_low, TN)
            grad_probs = dot(grad, v_win[keys, :], NT)
            grad_low = (probs_low.astype(jnp.float32) * (grad_probs - delta)).astype(jnp.bfloat16)
            dq_own[pl.ds(at, TILE), columns] = (dot(grad_low, k_win[keys, :], NN) * SCALE).astype(
                jnp.bfloat16
            )
            dk_sum[:, keys] += dot(query, grad_low, TN)
        for n in range(per_tile):
            send_home(1, dq_own, dq_hbm, wide, t * per_tile + n)
        for a, sums, rim, back, scale in (
            (0, dk_sum, rim_dk, back_dk, SCALE),
            (1, dv_sum, rim_dv, back_dv, None),
        ):
            rim[pl.ds(at, TILE), :] = summed(sums, at, scale).astype(jnp.bfloat16)
            pltpu.make_async_remote_copy(
                src_ref=rim.at[pl.ds(at, TILE), :],
                dst_ref=back.at[pl.ds(at, TILE), :],
                send_sem=back_send.at[a, t],
                recv_sem=back_recv.at[a, t],
                device_id=before,
                device_id_type=MESH,
            ).start()

    @pl.loop(0, tiles)
    def _(t):
        at = pl.multiple_of(t * TILE, TILE)
        for a, sums, back, own, target, scale in (
            (0, dk_sum, back_dk, dk_own, dk_hbm, SCALE),
            (1, dv_sum, back_dv, dv_own, dv_hbm, None),
        ):
            landed = back.at[pl.ds(at, TILE), :]
            pltpu.make_async_copy(landed, landed, back_recv.at[a, t]).wait()
            total = summed(sums, WINDOW + at, scale) + back[pl.ds(at, TILE), :].astype(jnp.float32)
            own[pl.ds(at, TILE), :] = total.astype(jnp.bfloat16)
            for n in range(per_tile):
                send_home(2 + a, own, target, HEAD_WIDTH, t * per_tile + n)

    for copy in sends:
        copy.wait_send()
    results = (
        (o_own, o_hbm, wide),
        (dq_own, dq_hbm, wide),
        (dk_own, dk_hbm, HEAD_WIDTH),
        (dv_own, dv_hbm, HEAD_WIDTH),
    )
    for a, rim in ((0, rim_dk), (1, rim_dv)):
        for t in range(tiles):
            sent = rim.at[pl.ds(t * TILE, TILE), :]
            pltpu.make_async_copy(sent, sent, back_send.at[a, t]).wait()
    for a, (source, target, width) in enumerate(results):
        for index in range(blocks):

            @pl.when(index != mine)
            def _():
                sent = source.at[block_rows(index), :]
                pltpu.make_async_copy(sent, sent, out_send.at[a, index]).wait()

        for h in range(blocks):
            landed = target.at[:, h * width : (h + 1) * width]
            pltpu.make_async_copy(landed, landed, out_recv.at[a, h]).wait()


def shards(rotated_query_rows, rotated_key_rows, value_matrix, output_gradient, doc_lengths):
    chips = lax.axis_size("head")
    block, query_columns = rotated_query_rows.shape
    key_columns = rotated_key_rows.shape[1]
    group = query_columns // key_columns
    blocks = 2 * chips
    rows = blocks * block
    tiles = rows // TILE
    wide = group * HEAD_WIDTH
    low = jnp.bfloat16
    hbm = pl.BlockSpec(memory_space=pl.ANY)
    return pl.pallas_call(
        functools.partial(kernel, chips, block, group),
        out_shape=(
            jax.ShapeDtypeStruct((block, query_columns), low),
            jax.ShapeDtypeStruct((block, query_columns), low),
            jax.ShapeDtypeStruct((block, key_columns), low),
            jax.ShapeDtypeStruct((block, key_columns), low),
        ),
        in_specs=[hbm] * 4 + [pl.BlockSpec(memory_space=pltpu.SMEM)],
        out_specs=(hbm,) * 4,
        scratch_shapes=[
            pltpu.VMEM((rows, wide), low),
            pltpu.VMEM((rows, wide), low),
            pltpu.VMEM((WINDOW + rows, HEAD_WIDTH), low),
            pltpu.VMEM((WINDOW + rows, HEAD_WIDTH), low),
            pltpu.VMEM((rows, wide), low),
            pltpu.VMEM((rows, wide), low),
            pltpu.VMEM((tiles, group * TILE, SPAN), low),
            pltpu.VMEM((rows, 128), jnp.int32),
            pltpu.VMEM((HEAD_WIDTH, WINDOW + rows), jnp.float32),
            pltpu.VMEM((HEAD_WIDTH, WINDOW + rows), jnp.float32),
            pltpu.VMEM((rows, HEAD_WIDTH), low),
            pltpu.VMEM((rows, HEAD_WIDTH), low),
            pltpu.VMEM((rows, HEAD_WIDTH), low),
            pltpu.VMEM((rows, HEAD_WIDTH), low),
            pltpu.VMEM((rows, HEAD_WIDTH), low),
            pltpu.VMEM((rows, HEAD_WIDTH), low),
            pltpu.SemaphoreType.DMA((4, blocks - 1)),
            pltpu.SemaphoreType.DMA((4, blocks)),
            pltpu.SemaphoreType.DMA((2, blocks)),
            pltpu.SemaphoreType.DMA((2, blocks)),
            pltpu.SemaphoreType.DMA((2, tiles)),
            pltpu.SemaphoreType.DMA((2, tiles)),
            pltpu.SemaphoreType.DMA((4, blocks)),
            pltpu.SemaphoreType.DMA((4, blocks)),
        ],
        compiler_params=pltpu.CompilerParams(
            collective_id=0, has_side_effects=True, vmem_limit_bytes=48 * 2**20
        ),
    )(rotated_query_rows, rotated_key_rows, value_matrix, output_gradient, doc_lengths)


def solution(mesh):
    rows = P(("seq", "head"), None)
    return jax.shard_map(
        shards,
        mesh=mesh,
        in_specs=(rows, rows, rows, rows, P()),
        out_specs=(rows, rows, rows, rows),
        check_vma=False,
    )
```

```python
import functools
import math

import jax
import jax.numpy as jnp
from jax import lax
from jax.experimental import pallas as pl
from jax.experimental.pallas import tpu as pltpu
from jax.sharding import PartitionSpec as P

MESH = pl.DeviceIdType.MESH
HEAD_WIDTH = 256
WINDOW = 1024
TILE = 256
SPAN = WINDOW + TILE
SCALE = HEAD_WIDTH ** -0.5
LOG2E = math.log2(math.e)
HIDDEN = -1e30
NT = (((1,), (1,)), ((), ()))
NN = (((1,), (0,)), ((), ()))
TN = (((0,), (0,)), ((), ()))


def dot(left, right, dims):
    return lax.dot_general(left, right, dims, preferred_element_type=jnp.float32)


def kernel(
    chips,
    block,
    group,
    q_hbm,
    k_hbm,
    v_hbm,
    g_hbm,
    lens,
    o_hbm,
    dq_hbm,
    dk_hbm,
    dv_hbm,
    q_own,
    g_own,
    k_win,
    v_win,
    o_own,
    dq_own,
    probs,
    first_key,
    dk_sum,
    dv_sum,
    rim_dk,
    rim_dv,
    back_dk,
    back_dv,
    dk_own,
    dv_own,
    in_send,
    in_recv,
    rim_send,
    rim_recv,
    back_send,
    back_recv,
    out_send,
    out_recv,
):
    blocks = 2 * chips
    rows = blocks * block
    tiles = rows // TILE
    per_tile = TILE // block
    wide = group * HEAD_WIDTH
    seq = lax.axis_index("seq")
    x = lax.axis_index("head")
    seqs = lax.axis_size("seq")
    core = lax.rem(seq, 2)
    row_base = seq - core
    mine = core * chips + x
    head = 2 * x + core
    after = (lax.rem(seq + 2, seqs), x)
    before = (lax.rem(seq + seqs - 2, seqs), x)
    has_after = seq + 2 < seqs
    has_before = seq >= 2

    peers = []
    for dx, dc in ((0, 1), (1, 0), (chips - 1, 0), (1, 1), (chips - 1, 1), (2, 0), (2, 1)):
        peer_core = lax.rem(core + dc, 2)
        peer_x = lax.rem(x + dx, chips)
        peers.append((row_base + peer_core, peer_x, peer_core * chips + peer_x, 2 * peer_x + peer_core))

    barrier = pltpu.get_barrier_semaphore()
    for peer in peers:
        pl.semaphore_signal(barrier, inc=1, device_id=(peer[0], peer[1]), device_id_type=MESH)

    @pl.when(has_after)
    def _():
        pl.semaphore_signal(barrier, inc=1, device_id=after, device_id_type=MESH)

    @pl.when(has_before)
    def _():
        pl.semaphore_signal(barrier, inc=1, device_id=before, device_id_type=MESH)

    def block_rows(index, offset=0):
        return pl.ds(pl.multiple_of(offset + index * block, block), block)

    def head_columns(index, width):
        return pl.ds(pl.multiple_of(index * width, width), width)

    moves = (
        (k_hbm, k_win, HEAD_WIDTH, WINDOW),
        (v_hbm, v_win, HEAD_WIDTH, WINDOW),
        (q_hbm, q_own, wide, 0),
        (g_hbm, g_own, wide, 0),
    )
    for a, (source, target, width, offset) in enumerate(moves):
        pltpu.make_async_copy(
            source.at[:, head_columns(head, width)],
            target.at[block_rows(mine, offset), :],
            in_recv.at[a, mine],
        ).start()

    place = (seq // 2) * rows + lax.broadcasted_iota(jnp.int32, (8, rows), 1)

    def next_doc(d, carry):
        start, first = carry
        return start + lens[d], jnp.where(place >= start, start, first)

    _, first = lax.fori_loop(
        0, lens.shape[0], next_doc, (jnp.int32(0), jnp.zeros((8, rows), jnp.int32))
    )
    in_row = lax.broadcasted_iota(jnp.int32, (8, rows), 1)
    tile_start = in_row // TILE * TILE
    first = jnp.maximum(first, place - (WINDOW - 1)) - (place - in_row - WINDOW) - tile_start
    first_key[...] = jnp.transpose(jnp.concatenate([first] * 16, axis=0))
    dk_sum[...] = jnp.zeros_like(dk_sum)
    dv_sum[...] = jnp.zeros_like(dv_sum)

    @pl.when(jnp.logical_not(has_before))
    def _():
        k_win[0:WINDOW, :] = jnp.zeros((WINDOW, HEAD_WIDTH), k_win.dtype)
        v_win[0:WINDOW, :] = jnp.zeros((WINDOW, HEAD_WIDTH), v_win.dtype)

    @pl.when(jnp.logical_not(has_after))
    def _():
        back_dk[...] = jnp.zeros_like(back_dk)
        back_dv[...] = jnp.zeros_like(back_dv)

    pl.semaphore_wait(barrier, len(peers) + has_after.astype(jnp.int32) + has_before.astype(jnp.int32))

    sends = []
    for a, (source, target, width, offset) in enumerate(moves):
        for n, peer in enumerate(peers):
            copy = pltpu.make_async_remote_copy(
                src_ref=source.at[:, head_columns(peer[3], width)],
                dst_ref=target.at[block_rows(mine, offset), :],
                send_sem=in_send.at[a, n],
                recv_sem=in_recv.at[a, mine],
                device_id=(peer[0], peer[1]),
                device_id_type=MESH,
            )
            copy.start()
            sends.append(copy)

    def arrived(a, index):
        source, target, width, offset = moves[a]
        landed = target.at[block_rows(index, offset), :]
        pltpu.make_async_copy(landed, landed, in_recv.at[a, index]).wait()

    for index in [mine] + [peer[2] for peer in peers]:
        for a, window in ((0, k_win), (1, v_win)):
            arrived(a, index)

            @pl.when(has_after)
            def _():
                pltpu.make_async_remote_copy(
                    src_ref=window.at[block_rows(index, WINDOW), :],
                    dst_ref=window.at[block_rows(index), :],
                    send_sem=rim_send.at[a, index],
                    recv_sem=rim_recv.at[a, index],
                    device_id=after,
                    device_id_type=MESH,
                ).start()

    for index in range(blocks):
        arrived(2, index)

    @pl.when(has_before)
    def _():
        for index in range(blocks):
            for a, window in ((0, k_win), (1, v_win)):
                landed = window.at[block_rows(index), :]
                pltpu.make_async_copy(landed, landed, rim_recv.at[a, index]).wait()

    def send_home(a, source, target, width, index):
        owner = (row_base + index // chips, lax.rem(index, chips))

        @pl.when(index == mine)
        def _():
            pltpu.make_async_copy(
                source.at[block_rows(index), :],
                target.at[:, head_columns(head, width)],
                out_recv.at[a, head],
            ).start()

        @pl.when(index != mine)
        def _():
            pltpu.make_async_remote_copy(
                src_ref=source.at[block_rows(index), :],
                dst_ref=target.at[:, head_columns(head, width)],
                send_sem=out_send.at[a, index],
                recv_sem=out_recv.at[a, head],
                device_id=owner,
                device_id_type=MESH,
            ).start()

    column = lax.broadcasted_iota(jnp.int32, (TILE, SPAN), 1)
    last_key = lax.broadcasted_iota(jnp.int32, (TILE, SPAN), 0) + WINDOW

    @pl.loop(0, tiles)
    def _(t):
        at = pl.multiple_of(t * TILE, TILE)
        keys = pl.ds(at, SPAN)
        for g in range(group):
            columns = slice(g * HEAD_WIDTH, (g + 1) * HEAD_WIDTH)
            scores = dot(q_own[pl.ds(at, TILE), columns], k_win[keys, :], NT)
            visible = (column >= first_key[pl.ds(at, TILE), 0:1]) & (column <= last_key)
            scores = jnp.where(visible, scores, HIDDEN)
            top = jnp.max(scores, axis=1, keepdims=True)
            weights = jnp.exp2((scores - top) * (SCALE * LOG2E))
            total = jnp.sum(weights, axis=1, keepdims=True)
            probs_low = (weights * (1.0 / total)).astype(jnp.bfloat16)
            probs[t, g * TILE : (g + 1) * TILE, :] = probs_low
            o_own[pl.ds(at, TILE), columns] = dot(probs_low, v_win[keys, :], NN).astype(jnp.bfloat16)
        for n in range(per_tile):
            send_home(0, o_own, o_hbm, wide, t * per_tile + n)

    for index in range(blocks):
        arrived(3, index)

    def summed(sums, chunk_start, scale):
        chunk = jnp.transpose(sums[:, pl.ds(chunk_start, TILE)])
        return chunk * scale if scale is not None else chunk

    @pl.loop(0, tiles)
    def _(t):
        at = pl.multiple_of(t * TILE, TILE)
        keys = pl.ds(at, SPAN)
        for g in range(group):
            columns = slice(g * HEAD_WIDTH, (g + 1) * HEAD_WIDTH)
            query = q_own[pl.ds(at, TILE), columns]
            grad = g_own[pl.ds(at, TILE), columns]
            low = o_own[pl.ds(at, TILE), columns]
            delta = jnp.sum(grad.astype(jnp.float32) * low.astype(jnp.float32), axis=1, keepdims=True)
            probs_low = probs[t, g * TILE : (g + 1) * TILE, :]
            dv_sum[:, keys] += dot(grad, probs_low, TN)
            grad_probs = dot(grad, v_win[keys, :], NT)
            grad_low = (probs_low.astype(jnp.float32) * (grad_probs - delta)).astype(jnp.bfloat16)
            dq_own[pl.ds(at, TILE), columns] = (dot(grad_low, k_win[keys, :], NN) * SCALE).astype(
                jnp.bfloat16
            )
            dk_sum[:, keys] += dot(query, grad_low, TN)
        for n in range(per_tile):
            send_home(1, dq_own, dq_hbm, wide, t * per_tile + n)
        for a, sums, rim, back, scale in (
            (0, dk_sum, rim_dk, back_dk, SCALE),
            (1, dv_sum, rim_dv, back_dv, None),
        ):
            rim[pl.ds(at, TILE), :] = summed(sums, at, scale).astype(jnp.bfloat16)

            @pl.when(has_before)
            def _():
                pltpu.make_async_remote_copy(
                    src_ref=rim.at[pl.ds(at, TILE), :],
                    dst_ref=back.at[pl.ds(at, TILE), :],
                    send_sem=back_send.at[a, t],
                    recv_sem=back_recv.at[a, t],
                    device_id=before,
                    device_id_type=MESH,
                ).start()

    @pl.loop(0, tiles)
    def _(t):
        at = pl.multiple_of(t * TILE, TILE)
        for a, sums, back, own, target, scale in (
            (0, dk_sum, back_dk, dk_own, dk_hbm, SCALE),
            (1, dv_sum, back_dv, dv_own, dv_hbm, None),
        ):

            @pl.when(has_after)
            def _():
                landed = back.at[pl.ds(at, TILE), :]
                pltpu.make_async_copy(landed, landed, back_recv.at[a, t]).wait()

            total = summed(sums, WINDOW + at, scale) + back[pl.ds(at, TILE), :].astype(jnp.float32)
            own[pl.ds(at, TILE), :] = total.astype(jnp.bfloat16)
            for n in range(per_tile):
                send_home(2 + a, own, target, HEAD_WIDTH, t * per_tile + n)

    for copy in sends:
        copy.wait_send()
    results = (
        (o_own, o_hbm, wide),
        (dq_own, dq_hbm, wide),
        (dk_own, dk_hbm, HEAD_WIDTH),
        (dv_own, dv_hbm, HEAD_WIDTH),
    )

    @pl.when(has_after)
    def _():
        for a, window in ((0, k_win), (1, v_win)):
            for index in range(blocks):
                sent = window.at[block_rows(index, WINDOW), :]
                pltpu.make_async_copy(sent, sent, rim_send.at[a, index]).wait()

    @pl.when(has_before)
    def _():
        for a, rim in ((0, rim_dk), (1, rim_dv)):
            for t in range(tiles):
                sent = rim.at[pl.ds(t * TILE, TILE), :]
                pltpu.make_async_copy(sent, sent, back_send.at[a, t]).wait()

    for a, (source, target, width) in enumerate(results):
        for index in range(blocks):

            @pl.when(index != mine)
            def _():
                sent = source.at[block_rows(index), :]
                pltpu.make_async_copy(sent, sent, out_send.at[a, index]).wait()

        for h in range(blocks):
            landed = target.at[:, h * width : (h + 1) * width]
            pltpu.make_async_copy(landed, landed, out_recv.at[a, h]).wait()


def land(*refs):
    half = len(refs) // 2
    sems = refs[-1]
    copies = [
        pltpu.make_async_copy(refs[n], refs[half + n], sems.at[n]) for n in range(half)
    ]
    for copy in copies:
        copy.start()
    for copy in copies:
        copy.wait()


def shards(rotated_query_rows, rotated_key_rows, value_matrix, output_gradient, doc_lengths):
    chips = lax.axis_size("head")
    block, query_columns = rotated_query_rows.shape
    key_columns = rotated_key_rows.shape[1]
    group = query_columns // key_columns
    blocks = 2 * chips
    rows = blocks * block
    tiles = rows // TILE
    wide = group * HEAD_WIDTH
    low = jnp.bfloat16
    hbm = pl.BlockSpec(memory_space=pl.ANY)
    shapes = (
        jax.ShapeDtypeStruct((block, query_columns), low),
        jax.ShapeDtypeStruct((block, query_columns), low),
        jax.ShapeDtypeStruct((block, key_columns), low),
        jax.ShapeDtypeStruct((block, key_columns), low),
    )
    results = pl.pallas_call(
        functools.partial(kernel, chips, block, group),
        out_shape=shapes,
        in_specs=[hbm] * 4 + [pl.BlockSpec(memory_space=pltpu.SMEM)],
        out_specs=(hbm,) * 4,
        scratch_shapes=[
            pltpu.VMEM((rows, wide), low),
            pltpu.VMEM((rows, wide), low),
            pltpu.VMEM((WINDOW + rows, HEAD_WIDTH), low),
            pltpu.VMEM((WINDOW + rows, HEAD_WIDTH), low),
            pltpu.VMEM((rows, wide), low),
            pltpu.VMEM((rows, wide), low),
            pltpu.VMEM((tiles, group * TILE, SPAN), low),
            pltpu.VMEM((rows, 128), jnp.int32),
            pltpu.VMEM((HEAD_WIDTH, WINDOW + rows), jnp.float32),
            pltpu.VMEM((HEAD_WIDTH, WINDOW + rows), jnp.float32),
            pltpu.VMEM((rows, HEAD_WIDTH), low),
            pltpu.VMEM((rows, HEAD_WIDTH), low),
            pltpu.VMEM((rows, HEAD_WIDTH), low),
            pltpu.VMEM((rows, HEAD_WIDTH), low),
            pltpu.VMEM((rows, HEAD_WIDTH), low),
            pltpu.VMEM((rows, HEAD_WIDTH), low),
            pltpu.SemaphoreType.DMA((4, blocks - 1)),
            pltpu.SemaphoreType.DMA((4, blocks)),
            pltpu.SemaphoreType.DMA((2, blocks)),
            pltpu.SemaphoreType.DMA((2, blocks)),
            pltpu.SemaphoreType.DMA((2, tiles)),
            pltpu.SemaphoreType.DMA((2, tiles)),
            pltpu.SemaphoreType.DMA((4, blocks)),
            pltpu.SemaphoreType.DMA((4, blocks)),
        ],
        compiler_params=pltpu.CompilerParams(
            collective_id=0, has_side_effects=True, vmem_limit_bytes=48 * 2**20
        ),
    )(
        *(
            pltpu.with_memory_space_constraint(array, pltpu.HBM)
            for array in (
                rotated_query_rows,
                rotated_key_rows,
                value_matrix,
                output_gradient,
                doc_lengths,
            )
        )
    )
    return pl.pallas_call(
        land,
        out_shape=tuple(pltpu.HBM(shape.shape, shape.dtype) for shape in shapes),
        in_specs=[hbm] * len(shapes),
        out_specs=(pl.BlockSpec(memory_space=pltpu.HBM),) * len(shapes),
        scratch_shapes=[pltpu.SemaphoreType.DMA((len(shapes),))],
        compiler_params=pltpu.CompilerParams(vmem_limit_bytes=2**20),
    )(*(pltpu.with_memory_space_constraint(result, pltpu.VMEM) for result in results))


def solution(mesh):
    rows = P(("seq", "head"), None)
    return jax.shard_map(
        shards,
        mesh=mesh,
        in_specs=(rows, rows, rows, rows, P()),
        out_specs=(rows, rows, rows, rows),
        check_vma=False,
    )
```

```python
import functools
import math

import jax
import jax.numpy as jnp
from jax import lax
from jax.experimental import pallas as pl
from jax.experimental.pallas import tpu as pltpu
from jax.sharding import PartitionSpec as P

MESH = pl.DeviceIdType.MESH
HEAD_WIDTH = 256
WINDOW = 1024
TILE = 256
SPAN = WINDOW + TILE
SCALE = HEAD_WIDTH ** -0.5
LOG2E = math.log2(math.e)
HIDDEN = -1e30
NT = (((1,), (1,)), ((), ()))
NN = (((1,), (0,)), ((), ()))
TN = (((0,), (0,)), ((), ()))


def dot(left, right, dims):
    return lax.dot_general(left, right, dims, preferred_element_type=jnp.float32)


def kernel(
    chips,
    block,
    group,
    q_hbm,
    k_hbm,
    v_hbm,
    g_hbm,
    lens,
    o_hbm,
    dq_hbm,
    dk_hbm,
    dv_hbm,
    q_here,
    k_here,
    v_here,
    g_here,
    q_own,
    g_own,
    k_win,
    v_win,
    o_own,
    dq_own,
    probs,
    first_key,
    dk_sum,
    dv_sum,
    rim_dk,
    rim_dv,
    back_dk,
    back_dv,
    dk_own,
    dv_own,
    here_sem,
    in_send,
    in_recv,
    rim_send,
    rim_recv,
    back_send,
    back_recv,
    out_send,
    out_recv,
):
    blocks = 2 * chips
    rows = blocks * block
    tiles = rows // TILE
    per_tile = TILE // block
    wide = group * HEAD_WIDTH
    seq = lax.axis_index("seq")
    x = lax.axis_index("head")
    seqs = lax.axis_size("seq")
    core = lax.rem(seq, 2)
    row_base = seq - core
    mine = core * chips + x
    head = 2 * x + core
    after = (lax.rem(seq + 2, seqs), x)
    before = (lax.rem(seq + seqs - 2, seqs), x)
    has_after = seq + 2 < seqs
    has_before = seq >= 2

    peers = []
    for dx, dc in ((0, 1), (2, 0), (2, 1), (1, 0), (chips - 1, 0), (1, 1), (chips - 1, 1)):
        peer_core = lax.rem(core + dc, 2)
        peer_x = lax.rem(x + dx, chips)
        peers.append((row_base + peer_core, peer_x, peer_core * chips + peer_x, 2 * peer_x + peer_core))

    barrier = pltpu.get_barrier_semaphore()
    for peer in peers:
        pl.semaphore_signal(barrier, inc=1, device_id=(peer[0], peer[1]), device_id_type=MESH)

    @pl.when(has_after)
    def _():
        pl.semaphore_signal(barrier, inc=1, device_id=after, device_id_type=MESH)

    @pl.when(has_before)
    def _():
        pl.semaphore_signal(barrier, inc=1, device_id=before, device_id_type=MESH)

    held = ((k_hbm, k_here), (v_hbm, v_here), (q_hbm, q_here), (g_hbm, g_here))
    for a, (source, target) in enumerate(held):
        pltpu.make_async_copy(source, target, here_sem.at[a]).start()

    def block_rows(index, offset=0):
        return pl.ds(pl.multiple_of(offset + index * block, block), block)

    def head_columns(index, width):
        return pl.ds(pl.multiple_of(index * width, width), width)

    moves = (
        (k_here, k_win, HEAD_WIDTH, WINDOW),
        (v_here, v_win, HEAD_WIDTH, WINDOW),
        (q_here, q_own, wide, 0),
        (g_here, g_own, wide, 0),
    )
    for a, (source, target, width, offset) in enumerate(moves):
        pltpu.make_async_copy(held[a][0], held[a][1], here_sem.at[a]).wait()
        pltpu.make_async_copy(
            source.at[:, head_columns(head, width)],
            target.at[block_rows(mine, offset), :],
            in_recv.at[a, mine],
        ).start()

    pl.semaphore_wait(barrier, len(peers) + has_after.astype(jnp.int32) + has_before.astype(jnp.int32))

    sends = []
    for a, (source, target, width, offset) in enumerate(moves):
        for n, peer in enumerate(peers):
            copy = pltpu.make_async_remote_copy(
                src_ref=source.at[:, head_columns(peer[3], width)],
                dst_ref=target.at[block_rows(mine, offset), :],
                send_sem=in_send.at[a, n],
                recv_sem=in_recv.at[a, mine],
                device_id=(peer[0], peer[1]),
                device_id_type=MESH,
            )
            copy.start()
            sends.append(copy)

    def arrived(a, index):
        source, target, width, offset = moves[a]
        landed = target.at[block_rows(index, offset), :]
        pltpu.make_async_copy(landed, landed, in_recv.at[a, index]).wait()

    for index in [mine] + [peer[2] for peer in peers]:
        for a, window in ((0, k_win), (1, v_win)):
            arrived(a, index)

            @pl.when(has_after)
            def _():
                pltpu.make_async_remote_copy(
                    src_ref=window.at[block_rows(index, WINDOW), :],
                    dst_ref=window.at[block_rows(index), :],
                    send_sem=rim_send.at[a, index],
                    recv_sem=rim_recv.at[a, index],
                    device_id=after,
                    device_id_type=MESH,
                ).start()

    place = (seq // 2) * rows + lax.broadcasted_iota(jnp.int32, (8, rows), 1)

    def next_doc(d, carry):
        start, first = carry
        return start + lens[d], jnp.where(place >= start, start, first)

    _, first = lax.fori_loop(
        0, lens.shape[0], next_doc, (jnp.int32(0), jnp.zeros((8, rows), jnp.int32))
    )
    in_row = lax.broadcasted_iota(jnp.int32, (8, rows), 1)
    tile_start = in_row // TILE * TILE
    first = jnp.maximum(first, place - (WINDOW - 1)) - (place - in_row - WINDOW) - tile_start
    first_key[...] = jnp.transpose(jnp.concatenate([first] * 16, axis=0))
    dk_sum[...] = jnp.zeros_like(dk_sum)
    dv_sum[...] = jnp.zeros_like(dv_sum)

    @pl.when(jnp.logical_not(has_before))
    def _():
        k_win[0:WINDOW, :] = jnp.zeros((WINDOW, HEAD_WIDTH), k_win.dtype)
        v_win[0:WINDOW, :] = jnp.zeros((WINDOW, HEAD_WIDTH), v_win.dtype)

    @pl.when(jnp.logical_not(has_after))
    def _():
        back_dk[...] = jnp.zeros_like(back_dk)
        back_dv[...] = jnp.zeros_like(back_dv)

    for index in range(blocks):
        arrived(2, index)

    @pl.when(has_before)
    def _():
        for index in range(blocks):
            for a, window in ((0, k_win), (1, v_win)):
                landed = window.at[block_rows(index), :]
                pltpu.make_async_copy(landed, landed, rim_recv.at[a, index]).wait()

    def send_home(a, source, target, width, index):
        owner = (row_base + index // chips, lax.rem(index, chips))

        @pl.when(index == mine)
        def _():
            pltpu.make_async_copy(
                source.at[block_rows(index), :],
                target.at[:, head_columns(head, width)],
                out_recv.at[a, head],
            ).start()

        @pl.when(index != mine)
        def _():
            pltpu.make_async_remote_copy(
                src_ref=source.at[block_rows(index), :],
                dst_ref=target.at[:, head_columns(head, width)],
                send_sem=out_send.at[a, index],
                recv_sem=out_recv.at[a, head],
                device_id=owner,
                device_id_type=MESH,
            ).start()

    column = lax.broadcasted_iota(jnp.int32, (TILE, SPAN), 1)
    last_key = lax.broadcasted_iota(jnp.int32, (TILE, SPAN), 0) + WINDOW

    @pl.loop(0, tiles)
    def _(t):
        at = pl.multiple_of(t * TILE, TILE)
        keys = pl.ds(at, SPAN)
        for g in range(group):
            columns = slice(g * HEAD_WIDTH, (g + 1) * HEAD_WIDTH)
            scores = dot(q_own[pl.ds(at, TILE), columns], k_win[keys, :], NT)
            visible = (column >= first_key[pl.ds(at, TILE), 0:1]) & (column <= last_key)
            scores = jnp.where(visible, scores, HIDDEN)
            top = jnp.max(scores, axis=1, keepdims=True)
            weights = jnp.exp2((scores - top) * (SCALE * LOG2E))
            total = jnp.sum(weights, axis=1, keepdims=True)
            probs_low = (weights * (1.0 / total)).astype(jnp.bfloat16)
            probs[t, g * TILE : (g + 1) * TILE, :] = probs_low
            o_own[pl.ds(at, TILE), columns] = dot(probs_low, v_win[keys, :], NN).astype(jnp.bfloat16)
        for n in range(per_tile):
            send_home(0, o_own, o_hbm, wide, t * per_tile + n)

    for index in range(blocks):
        arrived(3, index)

    def summed(sums, chunk_start, scale):
        chunk = jnp.transpose(sums[:, pl.ds(chunk_start, TILE)])
        return chunk * scale if scale is not None else chunk

    @pl.loop(0, tiles)
    def _(t):
        at = pl.multiple_of(t * TILE, TILE)
        keys = pl.ds(at, SPAN)
        for g in range(group):
            columns = slice(g * HEAD_WIDTH, (g + 1) * HEAD_WIDTH)
            query = q_own[pl.ds(at, TILE), columns]
            grad = g_own[pl.ds(at, TILE), columns]
            low = o_own[pl.ds(at, TILE), columns]
            delta = jnp.sum(grad.astype(jnp.float32) * low.astype(jnp.float32), axis=1, keepdims=True)
            probs_low = probs[t, g * TILE : (g + 1) * TILE, :]
            dv_sum[:, keys] += dot(grad, probs_low, TN)
            grad_probs = dot(grad, v_win[keys, :], NT)
            grad_low = (probs_low.astype(jnp.float32) * (grad_probs - delta)).astype(jnp.bfloat16)
            dq_own[pl.ds(at, TILE), columns] = (dot(grad_low, k_win[keys, :], NN) * SCALE).astype(
                jnp.bfloat16
            )
            dk_sum[:, keys] += dot(query, grad_low, TN)
        for n in range(per_tile):
            send_home(1, dq_own, dq_hbm, wide, t * per_tile + n)
        for a, sums, rim, back, scale in (
            (0, dk_sum, rim_dk, back_dk, SCALE),
            (1, dv_sum, rim_dv, back_dv, None),
        ):
            rim[pl.ds(at, TILE), :] = summed(sums, at, scale).astype(jnp.bfloat16)

            @pl.when(has_before)
            def _():
                pltpu.make_async_remote_copy(
                    src_ref=rim.at[pl.ds(at, TILE), :],
                    dst_ref=back.at[pl.ds(at, TILE), :],
                    send_sem=back_send.at[a, t],
                    recv_sem=back_recv.at[a, t],
                    device_id=before,
                    device_id_type=MESH,
                ).start()

    @pl.loop(0, tiles)
    def _(t):
        at = pl.multiple_of(t * TILE, TILE)
        for a, sums, back, own, target, scale in (
            (0, dk_sum, back_dk, dk_own, dk_hbm, SCALE),
            (1, dv_sum, back_dv, dv_own, dv_hbm, None),
        ):

            @pl.when(has_after)
            def _():
                landed = back.at[pl.ds(at, TILE), :]
                pltpu.make_async_copy(landed, landed, back_recv.at[a, t]).wait()

            total = summed(sums, WINDOW + at, scale) + back[pl.ds(at, TILE), :].astype(jnp.float32)
            own[pl.ds(at, TILE), :] = total.astype(jnp.bfloat16)
            for n in range(per_tile):
                send_home(2 + a, own, target, HEAD_WIDTH, t * per_tile + n)

    for copy in sends:
        copy.wait_send()
    results = (
        (o_own, o_hbm, wide),
        (dq_own, dq_hbm, wide),
        (dk_own, dk_hbm, HEAD_WIDTH),
        (dv_own, dv_hbm, HEAD_WIDTH),
    )

    @pl.when(has_after)
    def _():
        for a, window in ((0, k_win), (1, v_win)):
            for index in range(blocks):
                sent = window.at[block_rows(index, WINDOW), :]
                pltpu.make_async_copy(sent, sent, rim_send.at[a, index]).wait()

    @pl.when(has_before)
    def _():
        for a, rim in ((0, rim_dk), (1, rim_dv)):
            for t in range(tiles):
                sent = rim.at[pl.ds(t * TILE, TILE), :]
                pltpu.make_async_copy(sent, sent, back_send.at[a, t]).wait()

    for a, (source, target, width) in enumerate(results):
        for index in range(blocks):

            @pl.when(index != mine)
            def _():
                sent = source.at[block_rows(index), :]
                pltpu.make_async_copy(sent, sent, out_send.at[a, index]).wait()

        for h in range(blocks):
            landed = target.at[:, h * width : (h + 1) * width]
            pltpu.make_async_copy(landed, landed, out_recv.at[a, h]).wait()


def land(*refs):
    half = len(refs) // 2
    sems = refs[-1]
    copies = [
        pltpu.make_async_copy(refs[n], refs[half + n], sems.at[n]) for n in range(half)
    ]
    for copy in copies:
        copy.start()
    for copy in copies:
        copy.wait()


def shards(rotated_query_rows, rotated_key_rows, value_matrix, output_gradient, doc_lengths):
    chips = lax.axis_size("head")
    block, query_columns = rotated_query_rows.shape
    key_columns = rotated_key_rows.shape[1]
    group = query_columns // key_columns
    blocks = 2 * chips
    rows = blocks * block
    tiles = rows // TILE
    wide = group * HEAD_WIDTH
    low = jnp.bfloat16
    hbm = pl.BlockSpec(memory_space=pl.ANY)
    shapes = (
        jax.ShapeDtypeStruct((block, query_columns), low),
        jax.ShapeDtypeStruct((block, query_columns), low),
        jax.ShapeDtypeStruct((block, key_columns), low),
        jax.ShapeDtypeStruct((block, key_columns), low),
    )
    results = pl.pallas_call(
        functools.partial(kernel, chips, block, group),
        out_shape=shapes,
        in_specs=[hbm] * 4 + [pl.BlockSpec(memory_space=pltpu.SMEM)],
        out_specs=(hbm,) * 4,
        scratch_shapes=[
            pltpu.VMEM((block, query_columns), low),
            pltpu.VMEM((block, key_columns), low),
            pltpu.VMEM((block, key_columns), low),
            pltpu.VMEM((block, query_columns), low),
            pltpu.VMEM((rows, wide), low),
            pltpu.VMEM((rows, wide), low),
            pltpu.VMEM((WINDOW + rows, HEAD_WIDTH), low),
            pltpu.VMEM((WINDOW + rows, HEAD_WIDTH), low),
            pltpu.VMEM((rows, wide), low),
            pltpu.VMEM((rows, wide), low),
            pltpu.VMEM((tiles, group * TILE, SPAN), low),
            pltpu.VMEM((rows, 128), jnp.int32),
            pltpu.VMEM((HEAD_WIDTH, WINDOW + rows), jnp.float32),
            pltpu.VMEM((HEAD_WIDTH, WINDOW + rows), jnp.float32),
            pltpu.VMEM((rows, HEAD_WIDTH), low),
            pltpu.VMEM((rows, HEAD_WIDTH), low),
            pltpu.VMEM((rows, HEAD_WIDTH), low),
            pltpu.VMEM((rows, HEAD_WIDTH), low),
            pltpu.VMEM((rows, HEAD_WIDTH), low),
            pltpu.VMEM((rows, HEAD_WIDTH), low),
            pltpu.SemaphoreType.DMA((4,)),
            pltpu.SemaphoreType.DMA((4, blocks - 1)),
            pltpu.SemaphoreType.DMA((4, blocks)),
            pltpu.SemaphoreType.DMA((2, blocks)),
            pltpu.SemaphoreType.DMA((2, blocks)),
            pltpu.SemaphoreType.DMA((2, tiles)),
            pltpu.SemaphoreType.DMA((2, tiles)),
            pltpu.SemaphoreType.DMA((4, blocks)),
            pltpu.SemaphoreType.DMA((4, blocks)),
        ],
        compiler_params=pltpu.CompilerParams(
            collective_id=0, has_side_effects=True, vmem_limit_bytes=48 * 2**20
        ),
    )(
        *(
            pltpu.with_memory_space_constraint(array, pltpu.HBM)
            for array in (
                rotated_query_rows,
                rotated_key_rows,
                value_matrix,
                output_gradient,
                doc_lengths,
            )
        )
    )
    return pl.pallas_call(
        land,
        out_shape=tuple(pltpu.HBM(shape.shape, shape.dtype) for shape in shapes),
        in_specs=[hbm] * len(shapes),
        out_specs=(pl.BlockSpec(memory_space=pltpu.HBM),) * len(shapes),
        scratch_shapes=[pltpu.SemaphoreType.DMA((len(shapes),))],
        compiler_params=pltpu.CompilerParams(vmem_limit_bytes=2**20),
    )(*(pltpu.with_memory_space_constraint(result, pltpu.VMEM) for result in results))


def solution(mesh):
    rows = P(("seq", "head"), None)
    return jax.shard_map(
        shards,
        mesh=mesh,
        in_specs=(rows, rows, rows, rows, P()),
        out_specs=(rows, rows, rows, rows),
        check_vma=False,
    )
```

```python
import functools
import math

import jax
import jax.numpy as jnp
from jax import lax
from jax.experimental import pallas as pl
from jax.experimental.pallas import tpu as pltpu
from jax.sharding import PartitionSpec as P

MESH = pl.DeviceIdType.MESH
HEAD_WIDTH = 256
WINDOW = 1024
TILE = 256
SPAN = WINDOW + TILE
SCALE = HEAD_WIDTH ** -0.5
LOG2E = math.log2(math.e)
HIDDEN = -1e30
NT = (((1,), (1,)), ((), ()))
NN = (((1,), (0,)), ((), ()))
TN = (((0,), (0,)), ((), ()))


def dot(left, right, dims):
    return lax.dot_general(left, right, dims, preferred_element_type=jnp.float32)


def kernel(
    chips,
    block,
    group,
    q_hbm,
    k_hbm,
    v_hbm,
    g_hbm,
    lens,
    o_hbm,
    dq_hbm,
    dk_hbm,
    dv_hbm,
    q_here,
    k_here,
    v_here,
    g_here,
    q_own,
    g_own,
    k_win,
    v_win,
    o_own,
    dq_own,
    probs,
    first_key,
    dk_sum,
    dv_sum,
    rim_dk,
    rim_dv,
    back_dk,
    back_dv,
    dk_own,
    dv_own,
    here_sem,
    in_send,
    in_recv,
    rim_send,
    rim_recv,
    back_send,
    back_recv,
    out_send,
    out_recv,
):
    blocks = 2 * chips
    rows = blocks * block
    tiles = rows // TILE
    per_tile = TILE // block
    wide = group * HEAD_WIDTH
    seq = lax.axis_index("seq")
    x = lax.axis_index("head")
    seqs = lax.axis_size("seq")
    core = lax.rem(seq, 2)
    row_base = seq - core
    mine = core * chips + x
    head = 2 * x + core
    after = (lax.rem(seq + 2, seqs), x)
    before = (lax.rem(seq + seqs - 2, seqs), x)
    has_after = seq + 2 < seqs
    has_before = seq >= 2

    peers = []
    for dx, dc in ((0, 1), (2, 0), (2, 1), (1, 0), (chips - 1, 0), (1, 1), (chips - 1, 1)):
        peer_core = lax.rem(core + dc, 2)
        peer_x = lax.rem(x + dx, chips)
        peers.append((row_base + peer_core, peer_x, peer_core * chips + peer_x, 2 * peer_x + peer_core))

    barrier = pltpu.get_barrier_semaphore()
    for peer in peers[1:] + peers[:1]:
        pl.semaphore_signal(barrier, inc=1, device_id=(peer[0], peer[1]), device_id_type=MESH)

    @pl.when(has_after)
    def _():
        pl.semaphore_signal(barrier, inc=1, device_id=after, device_id_type=MESH)

    @pl.when(has_before)
    def _():
        pl.semaphore_signal(barrier, inc=1, device_id=before, device_id_type=MESH)

    held = ((k_hbm, k_here), (v_hbm, v_here), (q_hbm, q_here), (g_hbm, g_here))
    for a, (source, target) in enumerate(held):
        pltpu.make_async_copy(source, target, here_sem.at[a]).start()

    def block_rows(index, offset=0):
        return pl.ds(pl.multiple_of(offset + index * block, block), block)

    def head_columns(index, width):
        return pl.ds(pl.multiple_of(index * width, width), width)

    moves = (
        (k_here, k_win, HEAD_WIDTH, WINDOW),
        (v_here, v_win, HEAD_WIDTH, WINDOW),
        (q_here, q_own, wide, 0),
        (g_here, g_own, wide, 0),
    )
    for a, (source, target, width, offset) in enumerate(moves):
        pltpu.make_async_copy(held[a][0], held[a][1], here_sem.at[a]).wait()
        pltpu.make_async_copy(
            source.at[:, head_columns(head, width)],
            target.at[block_rows(mine, offset), :],
            in_recv.at[a, mine],
        ).start()

    pl.semaphore_wait(barrier, len(peers) + has_after.astype(jnp.int32) + has_before.astype(jnp.int32))

    sends = []
    for a, (source, target, width, offset) in enumerate(moves):
        for n, peer in list(enumerate(peers))[1:] + [(0, peers[0])]:
            copy = pltpu.make_async_remote_copy(
                src_ref=source.at[:, head_columns(peer[3], width)],
                dst_ref=target.at[block_rows(mine, offset), :],
                send_sem=in_send.at[a, n],
                recv_sem=in_recv.at[a, mine],
                device_id=(peer[0], peer[1]),
                device_id_type=MESH,
            )
            copy.start()
            sends.append(copy)

    def arrived(a, index):
        source, target, width, offset = moves[a]
        landed = target.at[block_rows(index, offset), :]
        pltpu.make_async_copy(landed, landed, in_recv.at[a, index]).wait()

    for index in [mine] + [peer[2] for peer in peers]:
        for a, window in ((0, k_win), (1, v_win)):
            arrived(a, index)

            @pl.when(has_after)
            def _():
                pltpu.make_async_remote_copy(
                    src_ref=window.at[block_rows(index, WINDOW), :],
                    dst_ref=window.at[block_rows(index), :],
                    send_sem=rim_send.at[a, index],
                    recv_sem=rim_recv.at[a, index],
                    device_id=after,
                    device_id_type=MESH,
                ).start()

    place = (seq // 2) * rows + lax.broadcasted_iota(jnp.int32, (8, rows), 1)

    def next_doc(d, carry):
        start, first = carry
        return start + lens[d], jnp.where(place >= start, start, first)

    _, first = lax.fori_loop(
        0, lens.shape[0], next_doc, (jnp.int32(0), jnp.zeros((8, rows), jnp.int32))
    )
    in_row = lax.broadcasted_iota(jnp.int32, (8, rows), 1)
    tile_start = in_row // TILE * TILE
    first = jnp.maximum(first, place - (WINDOW - 1)) - (place - in_row - WINDOW) - tile_start
    first_key[...] = jnp.transpose(jnp.concatenate([first] * 16, axis=0))
    dk_sum[...] = jnp.zeros_like(dk_sum)
    dv_sum[...] = jnp.zeros_like(dv_sum)

    @pl.when(jnp.logical_not(has_before))
    def _():
        k_win[0:WINDOW, :] = jnp.zeros((WINDOW, HEAD_WIDTH), k_win.dtype)
        v_win[0:WINDOW, :] = jnp.zeros((WINDOW, HEAD_WIDTH), v_win.dtype)

    @pl.when(jnp.logical_not(has_after))
    def _():
        back_dk[...] = jnp.zeros_like(back_dk)
        back_dv[...] = jnp.zeros_like(back_dv)

    for index in range(blocks):
        arrived(2, index)

    @pl.when(has_before)
    def _():
        for index in range(blocks):
            for a, window in ((0, k_win), (1, v_win)):
                landed = window.at[block_rows(index), :]
                pltpu.make_async_copy(landed, landed, rim_recv.at[a, index]).wait()

    def send_home(a, source, target, width, index):
        owner = (row_base + index // chips, lax.rem(index, chips))

        @pl.when(index == mine)
        def _():
            pltpu.make_async_copy(
                source.at[block_rows(index), :],
                target.at[:, head_columns(head, width)],
                out_recv.at[a, head],
            ).start()

        @pl.when(index != mine)
        def _():
            pltpu.make_async_remote_copy(
                src_ref=source.at[block_rows(index), :],
                dst_ref=target.at[:, head_columns(head, width)],
                send_sem=out_send.at[a, index],
                recv_sem=out_recv.at[a, head],
                device_id=owner,
                device_id_type=MESH,
            ).start()

    column = lax.broadcasted_iota(jnp.int32, (TILE, SPAN), 1)
    last_key = lax.broadcasted_iota(jnp.int32, (TILE, SPAN), 0) + WINDOW

    @pl.loop(0, tiles)
    def _(t):
        at = pl.multiple_of(t * TILE, TILE)
        keys = pl.ds(at, SPAN)
        for g in range(group):
            columns = slice(g * HEAD_WIDTH, (g + 1) * HEAD_WIDTH)
            scores = dot(q_own[pl.ds(at, TILE), columns], k_win[keys, :], NT)
            visible = (column >= first_key[pl.ds(at, TILE), 0:1]) & (column <= last_key)
            scores = jnp.where(visible, scores, HIDDEN)
            top = jnp.max(scores, axis=1, keepdims=True)
            weights = jnp.exp2((scores - top) * (SCALE * LOG2E))
            total = jnp.sum(weights, axis=1, keepdims=True)
            probs_low = (weights * (1.0 / total)).astype(jnp.bfloat16)
            probs[t, g * TILE : (g + 1) * TILE, :] = probs_low
            o_own[pl.ds(at, TILE), columns] = dot(probs_low, v_win[keys, :], NN).astype(jnp.bfloat16)
        for n in range(per_tile):
            send_home(0, o_own, o_hbm, wide, t * per_tile + n)

    for index in range(blocks):
        arrived(3, index)

    def summed(sums, chunk_start, scale):
        chunk = jnp.transpose(sums[:, pl.ds(chunk_start, TILE)])
        return chunk * scale if scale is not None else chunk

    @pl.loop(0, tiles)
    def _(t):
        at = pl.multiple_of(t * TILE, TILE)
        keys = pl.ds(at, SPAN)
        for g in range(group):
            columns = slice(g * HEAD_WIDTH, (g + 1) * HEAD_WIDTH)
            query = q_own[pl.ds(at, TILE), columns]
            grad = g_own[pl.ds(at, TILE), columns]
            low = o_own[pl.ds(at, TILE), columns]
            delta = jnp.sum(grad.astype(jnp.float32) * low.astype(jnp.float32), axis=1, keepdims=True)
            probs_low = probs[t, g * TILE : (g + 1) * TILE, :]
            dv_sum[:, keys] += dot(grad, probs_low, TN)
            grad_probs = dot(grad, v_win[keys, :], NT)
            grad_low = (probs_low.astype(jnp.float32) * (grad_probs - delta)).astype(jnp.bfloat16)
            dq_own[pl.ds(at, TILE), columns] = (dot(grad_low, k_win[keys, :], NN) * SCALE).astype(
                jnp.bfloat16
            )
            dk_sum[:, keys] += dot(query, grad_low, TN)
        for n in range(per_tile):
            send_home(1, dq_own, dq_hbm, wide, t * per_tile + n)
        for a, sums, rim, back, scale in (
            (0, dk_sum, rim_dk, back_dk, SCALE),
            (1, dv_sum, rim_dv, back_dv, None),
        ):
            rim[pl.ds(at, TILE), :] = summed(sums, at, scale).astype(jnp.bfloat16)

            @pl.when(has_before)
            def _():
                pltpu.make_async_remote_copy(
                    src_ref=rim.at[pl.ds(at, TILE), :],
                    dst_ref=back.at[pl.ds(at, TILE), :],
                    send_sem=back_send.at[a, t],
                    recv_sem=back_recv.at[a, t],
                    device_id=before,
                    device_id_type=MESH,
                ).start()

    @pl.loop(0, tiles)
    def _(t):
        at = pl.multiple_of(t * TILE, TILE)
        for a, sums, back, own, target, scale in (
            (0, dk_sum, back_dk, dk_own, dk_hbm, SCALE),
            (1, dv_sum, back_dv, dv_own, dv_hbm, None),
        ):

            @pl.when(has_after)
            def _():
                landed = back.at[pl.ds(at, TILE), :]
                pltpu.make_async_copy(landed, landed, back_recv.at[a, t]).wait()

            total = summed(sums, WINDOW + at, scale) + back[pl.ds(at, TILE), :].astype(jnp.float32)
            own[pl.ds(at, TILE), :] = total.astype(jnp.bfloat16)
            for n in range(per_tile):
                send_home(2 + a, own, target, HEAD_WIDTH, t * per_tile + n)

    for copy in sends:
        copy.wait_send()
    results = (
        (o_own, o_hbm, wide),
        (dq_own, dq_hbm, wide),
        (dk_own, dk_hbm, HEAD_WIDTH),
        (dv_own, dv_hbm, HEAD_WIDTH),
    )

    @pl.when(has_after)
    def _():
        for a, window in ((0, k_win), (1, v_win)):
            for index in range(blocks):
                sent = window.at[block_rows(index, WINDOW), :]
                pltpu.make_async_copy(sent, sent, rim_send.at[a, index]).wait()

    @pl.when(has_before)
    def _():
        for a, rim in ((0, rim_dk), (1, rim_dv)):
            for t in range(tiles):
                sent = rim.at[pl.ds(t * TILE, TILE), :]
                pltpu.make_async_copy(sent, sent, back_send.at[a, t]).wait()

    for a, (source, target, width) in enumerate(results):
        for index in range(blocks):

            @pl.when(index != mine)
            def _():
                sent = source.at[block_rows(index), :]
                pltpu.make_async_copy(sent, sent, out_send.at[a, index]).wait()

        for h in range(blocks):
            landed = target.at[:, h * width : (h + 1) * width]
            pltpu.make_async_copy(landed, landed, out_recv.at[a, h]).wait()


def land(*refs):
    half = len(refs) // 2
    sems = refs[-1]
    copies = [
        pltpu.make_async_copy(refs[n], refs[half + n], sems.at[n]) for n in range(half)
    ]
    for copy in copies:
        copy.start()
    for copy in copies:
        copy.wait()


def shards(rotated_query_rows, rotated_key_rows, value_matrix, output_gradient, doc_lengths):
    chips = lax.axis_size("head")
    block, query_columns = rotated_query_rows.shape
    key_columns = rotated_key_rows.shape[1]
    group = query_columns // key_columns
    blocks = 2 * chips
    rows = blocks * block
    tiles = rows // TILE
    wide = group * HEAD_WIDTH
    low = jnp.bfloat16
    hbm = pl.BlockSpec(memory_space=pl.ANY)
    shapes = (
        jax.ShapeDtypeStruct((block, query_columns), low),
        jax.ShapeDtypeStruct((block, query_columns), low),
        jax.ShapeDtypeStruct((block, key_columns), low),
        jax.ShapeDtypeStruct((block, key_columns), low),
    )
    results = pl.pallas_call(
        functools.partial(kernel, chips, block, group),
        out_shape=shapes,
        in_specs=[hbm] * 4 + [pl.BlockSpec(memory_space=pltpu.SMEM)],
        out_specs=(hbm,) * 4,
        scratch_shapes=[
            pltpu.VMEM((block, query_columns), low),
            pltpu.VMEM((block, key_columns), low),
            pltpu.VMEM((block, key_columns), low),
            pltpu.VMEM((block, query_columns), low),
            pltpu.VMEM((rows, wide), low),
            pltpu.VMEM((rows, wide), low),
            pltpu.VMEM((WINDOW + rows, HEAD_WIDTH), low),
            pltpu.VMEM((WINDOW + rows, HEAD_WIDTH), low),
            pltpu.VMEM((rows, wide), low),
            pltpu.VMEM((rows, wide), low),
            pltpu.VMEM((tiles, group * TILE, SPAN), low),
            pltpu.VMEM((rows, 128), jnp.int32),
            pltpu.VMEM((HEAD_WIDTH, WINDOW + rows), jnp.float32),
            pltpu.VMEM((HEAD_WIDTH, WINDOW + rows), jnp.float32),
            pltpu.VMEM((rows, HEAD_WIDTH), low),
            pltpu.VMEM((rows, HEAD_WIDTH), low),
            pltpu.VMEM((rows, HEAD_WIDTH), low),
            pltpu.VMEM((rows, HEAD_WIDTH), low),
            pltpu.VMEM((rows, HEAD_WIDTH), low),
            pltpu.VMEM((rows, HEAD_WIDTH), low),
            pltpu.SemaphoreType.DMA((4,)),
            pltpu.SemaphoreType.DMA((4, blocks - 1)),
            pltpu.SemaphoreType.DMA((4, blocks)),
            pltpu.SemaphoreType.DMA((2, blocks)),
            pltpu.SemaphoreType.DMA((2, blocks)),
            pltpu.SemaphoreType.DMA((2, tiles)),
            pltpu.SemaphoreType.DMA((2, tiles)),
            pltpu.SemaphoreType.DMA((4, blocks)),
            pltpu.SemaphoreType.DMA((4, blocks)),
        ],
        compiler_params=pltpu.CompilerParams(
            collective_id=0, has_side_effects=True, vmem_limit_bytes=48 * 2**20
        ),
    )(
        *(
            pltpu.with_memory_space_constraint(array, pltpu.HBM)
            for array in (
                rotated_query_rows,
                rotated_key_rows,
                value_matrix,
                output_gradient,
                doc_lengths,
            )
        )
    )
    return pl.pallas_call(
        land,
        out_shape=tuple(pltpu.HBM(shape.shape, shape.dtype) for shape in shapes),
        in_specs=[hbm] * len(shapes),
        out_specs=(pl.BlockSpec(memory_space=pltpu.HBM),) * len(shapes),
        scratch_shapes=[pltpu.SemaphoreType.DMA((len(shapes),))],
        compiler_params=pltpu.CompilerParams(vmem_limit_bytes=2**20),
    )(*(pltpu.with_memory_space_constraint(result, pltpu.VMEM) for result in results))


def solution(mesh):
    rows = P(("seq", "head"), None)
    return jax.shard_map(
        shards,
        mesh=mesh,
        in_specs=(rows, rows, rows, rows, P()),
        out_specs=(rows, rows, rows, rows),
        check_vma=False,
    )
```
